256 devices in a mesh: section: 32 (over y, z), dp: 8 (over x, core).
Axes of the slice: x: 4, y: 4, z: 8, core: 2. Of those that a mesh axis runs over, the one named last changes fastest.
Arguments:
- w_first: bfloat16 [32, 512, 2048], P('section'), may hold values from -0.25 to 0.25
- w_second_t: bfloat16 [32, 512, 2048], P('section'), may hold values from -0.125 to 0.125
- m_first: float32 [32, 512, 2048], P('section', 'dp'), may hold values from -6 to 6
- v_first: float32 [32, 512, 2048], P('section', 'dp'), may hold values from 10 to 100
- m_second: float32 [32, 512, 2048], P('section', 'dp'), may hold values from -6 to 6
- v_second: float32 [32, 512, 2048], P('section', 'dp'), may hold values from 10 to 100
- lengths: int32 [8, 34], replicated, may hold values from 1 to 256, 4352 in all within a row
- act_arrive: bfloat16 [8, 32, 256, 512], P('dp', 'section'), may hold values from -6 to 6
- cot_arrive: bfloat16 [8, 32, 256, 512], P('dp', 'section'), may hold values from -6 to 6
- embed_next: bfloat16 [8, 2, 256, 512], P('dp'), may hold values from -6 to 6
- loss_cot: bfloat16 [8, 2, 256, 512], P('dp'), may hold values from -6 to 6
- stash: bfloat16 [8, 32, 3, 256, 512], P('dp', 'section'), may hold values from -6 to 6
Outputs:
- act_leave: bfloat16 [8, 32, 3, 256, 512], P('dp', 'section')
- cot_leave: bfloat16 [8, 32, 3, 256, 512], P('dp', 'section')
- step_first: float32 [32, 512, 2048], P('section', 'dp')
- step_second: float32 [32, 512, 2048], P('section', 'dp')
The draws below stay inside these ranges and needn't reach their ends.
Inputs may be any that keep to these rules, and one draw needn't show every extreme that they name: lengths[g, m] counts the live rows of microbatch m of data group g; each row of lengths sums to 4352 and its largest entry is 256.
All inputs are finite; a program needn't handle non-finite values.
Results may differ from the reference program's by a relative error of at most 0.007.
Values may be sent and summed in bfloat16 or wider, within the bound.
No kernel may reach another device: no remote copies, remote signals or barrier semaphores. Data moves between devices by JAX's collectives and lax.ppermute only.
A program may use at most 128 MiB of HBM per device.

```python
import math
import jax
import jax.numpy as jnp
import numpy as np
from jax import lax

D = 512
FF = 2048
CAP = 256
TICKS = 3
SECTIONS = 32
GROUPS = 8
MB = 34
LEN_MEAN = 128


def shard_levels(key, shape, pieces, smallest, high):
    factor_of = 1.0
    for dim, shards_of in pieces:
        heights = jax.random.uniform(jax.random.fold_in(jax.random.fold_in(key, 6), dim), (shards_of,), jnp.float32, smallest / len(pieces), high / len(pieces))
        factor_of = factor_of * jnp.repeat(jnp.exp(heights), shape[dim] // shards_of).reshape((-1,) + (1,) * (len(shape) - 1 - dim))
    return factor_of


def split_up(count, total, most, slope):
    portions = [(1 << 20) // math.isqrt(standing ** slope) + 1 for standing in range(2, count + 1)]
    rest, counts = total - most - (count - 1), [1] * (count - 1)
    while rest > 0:
        candidates = [i for i in range(count - 1) if counts[i] < most]
        whole, budget = sum([portions[i] for i in candidates]), rest
        for i in candidates:
            addition = min(most - counts[i], max(1, budget * portions[i] // whole), rest)
            counts[i] = counts[i] + addition
            rest = rest - addition
    return np.array([most] + counts)


def ragged(stream_key, amount, total, most, slope):
    if amount == 2:
        one = jax.random.randint(stream_key, (), max(1, total - most), min(most, total - 1) + 1)
        return jnp.stack([one, total - one])
    tallies = jnp.asarray(split_up(amount, total, most, slope), jnp.int32)
    pairs = (amount - 1) // 2
    source_of, taker = tallies[1:1 + 2 * pairs:2], tallies[2:2 + 2 * pairs:2]
    slack = jnp.minimum(source_of - 1, most - taker)
    passed = jax.random.randint(jax.random.fold_in(stream_key, 1), (pairs,), 0, 1 << 20) % (slack + 1)
    tallies = tallies.at[1:1 + 2 * pairs:2].set(source_of - passed).at[2:2 + 2 * pairs:2].set(taker + passed)
    return tallies[jax.random.permutation(jax.random.fold_in(stream_key, 2), amount)]


def bell_draw(rng, shape, spread, bound, shards=(), kind=jnp.bfloat16):
    result = spread * jax.random.normal(rng, shape, jnp.float32)
    if shards:
        result = result * shard_levels(rng, shape, shards, -0.22, 0.18)
    return jnp.clip(result, -bound, bound).astype(kind)


def setup_inputs(seed: int = 0) -> dict:
    keys = jax.random.split(jax.random.key(seed), 13)
    w_first = bell_draw(keys[0], (SECTIONS, D, FF), D ** -0.5, 0.25, ((0, 32),))
    w_second_t = bell_draw(keys[1], (SECTIONS, D, FF), FF ** -0.5, 0.125, ((0, 32),))
    m_first = bell_draw(keys[2], (SECTIONS, D, FF), 1.0, 6.0, ((0, 32), (1, 8)), jnp.float32)
    v_first = jnp.clip(jnp.exp(math.log(100.0) - 2.3025851 * jax.random.uniform(keys[3], (SECTIONS, D, FF), jnp.float32) ** shard_levels(keys[3], (SECTIONS, D, FF), ((0, 32), (1, 8)), -0.2, 0.2)), 10.0, 100.0)
    m_second = bell_draw(keys[4], (SECTIONS, D, FF), 1.0, 6.0, ((0, 32), (1, 8)), jnp.float32)
    v_second = jnp.clip(jnp.exp(math.log(100.0) - 2.3025851 * jax.random.uniform(keys[5], (SECTIONS, D, FF), jnp.float32) ** shard_levels(keys[5], (SECTIONS, D, FF), ((0, 32), (1, 8)), -0.2, 0.2)), 10.0, 100.0)
    lengths = jax.vmap(lambda own: ragged(own, MB, LEN_MEAN * MB, CAP, 2))(jax.random.split(keys[6], GROUPS)).reshape((GROUPS, MB)).astype(jnp.int32)
    act_arrive = bell_draw(keys[7], (GROUPS, SECTIONS, CAP, D), 1.0, 6.0, ((0, 8), (1, 32)))
    cot_arrive = bell_draw(keys[8], (GROUPS, SECTIONS, CAP, D), 1.0, 6.0, ((0, 8), (1, 32)))
    embed_next = bell_draw(keys[9], (GROUPS, TICKS - 1, CAP, D), 1.0, 6.0, ((0, 8),))
    loss_cot = bell_draw(keys[10], (GROUPS, TICKS - 1, CAP, D), 1.0, 6.0, ((0, 8),))
    stash = bell_draw(keys[11], (GROUPS, SECTIONS, TICKS, CAP, D), 1.0, 6.0, ((0, 8), (1, 32)))
    return {"w_first": w_first, "w_second_t": w_second_t, "m_first": m_first, "v_first": v_first, "m_second": m_second, "v_second": v_second, "lengths": lengths, "act_arrive": act_arrive, "cot_arrive": cot_arrive, "embed_next": embed_next, "loss_cot": loss_cot, "stash": stash}


NORM_EPS = 1e-05
ADAM_EPS = 1e-08
beta_one = 0.9
beta_two = 0.98
correct_one = 1.0 - 0.9 ** 10
correct_two = 1.0 - 0.98 ** 10
gelu_coeff = 0.7978845608
cubic_coeff = 0.044715
residual_alpha = 1500.0 ** 0.25
contract_rows = (((0,), (0,)), ((), ()))
contract_cols = (((1,), (1,)), ((), ()))

def gelu_parts(pre_act):
    inner_arg = gelu_coeff * (pre_act + cubic_coeff * pre_act * pre_act * pre_act)
    tangent = jnp.tanh(inner_arg)
    gelu_value = 0.5 * pre_act * (1.0 + tangent)
    gelu_slope = 0.5 * (1.0 + tangent) + 0.5 * pre_act * (1.0 - tangent * tangent) * gelu_coeff * (1.0 + 3.0 * cubic_coeff * pre_act * pre_act)
    return (gelu_value, gelu_slope)

def layer_forward(inputs, weight_first, weight_second, residual_scale):
    pre_act = jnp.dot(inputs, weight_first, preferred_element_type=jnp.float32)
    gelu_value, gelu_slope = gelu_parts(pre_act)
    hidden = gelu_value.astype(jnp.bfloat16)
    branch = lax.dot_general(hidden, weight_second, contract_cols, preferred_element_type=jnp.float32)
    summed = residual_scale * inputs.astype(jnp.float32) + branch
    center = summed - lax.optimization_barrier(jnp.mean(summed, axis=1, keepdims=True))
    inv_std = lax.rsqrt(lax.optimization_barrier(jnp.mean(center * center, axis=1, keepdims=True)) + NORM_EPS)
    return (gelu_slope, hidden, center * inv_std, inv_std)

def live_mask(inputs, length, first_row):
    return lax.broadcasted_iota(jnp.int32, (inputs.shape[0], 1), 0) + first_row < length

def section_forward(inputs, weight_first, weight_second, length, first_row, residual_scale):
    normed = layer_forward(inputs, weight_first, weight_second, residual_scale)[2]
    return jnp.where(live_mask(inputs, length, first_row), normed, 0.0).astype(jnp.bfloat16)

def section_backward(inputs, cotangent, weight_first, weight_second, length, first_row, residual_scale):
    gelu_slope, hidden, normed, inv_std = layer_forward(inputs, weight_first, weight_second, residual_scale)
    grad_out = jnp.where(live_mask(inputs, length, first_row), cotangent.astype(jnp.float32), 0.0)
    grad_sum = inv_std * (grad_out - lax.optimization_barrier(jnp.mean(grad_out, axis=1, keepdims=True)) - normed * lax.optimization_barrier(jnp.mean(grad_out * normed, axis=1, keepdims=True)))
    grad_sum_b = grad_sum.astype(jnp.bfloat16)
    grad_hidden = jnp.dot(grad_sum_b, weight_second, preferred_element_type=jnp.float32)
    grad_pre = (grad_hidden * gelu_slope).astype(jnp.bfloat16)
    grad_in = (residual_scale * grad_sum + lax.dot_general(grad_pre, weight_first, contract_cols, preferred_element_type=jnp.float32)).astype(jnp.bfloat16)
    return (grad_in, grad_pre, grad_sum_b, hidden)

def adam_step(gradient, moment, second):
    moment_new = beta_one * moment + (1.0 - beta_one) * gradient
    second_new = beta_two * second + (1.0 - beta_two) * gradient * gradient
    return moment_new / correct_one / (jnp.sqrt(second_new / correct_two) + ADAM_EPS)

def reference(w_first, w_second_t, m_first, v_first, m_second, v_second, lengths, act_arrive, cot_arrive, embed_next, loss_cot, stash):
    residual_scale = residual_alpha
    sections = jnp.arange(SECTIONS, dtype=jnp.int32)

    def forward_item(section_item):
        return section_forward(section_item[0], section_item[1], section_item[2], section_item[3], 0, residual_scale)

    def backward_item(section_item):
        saved_in, cot_in, weight_first, weight_second, length = section_item
        grad_in, grad_pre, grad_sum_b, hidden = section_backward(saved_in, cot_in, weight_first, weight_second, length, 0, residual_scale)
        term_first = lax.dot_general(saved_in, grad_pre, contract_rows, preferred_element_type=jnp.float32)
        term_second = lax.dot_general(grad_sum_b, hidden, contract_rows, preferred_element_type=jnp.float32)
        return (grad_in, term_first, term_second)

    def one_group(sums_carry, group_data):
        group_lengths, arrive_rows, embeds, cot_rows, losses, saved_inputs = group_data
        inputs = arrive_rows
        forward_outs = []
        for tick_index in range(TICKS):
            tick_lengths = group_lengths[tick_index - sections + SECTIONS - 1]
            outputs = lax.map(forward_item, (inputs, w_first, w_second_t, tick_lengths))
            forward_outs.append(outputs)
            if tick_index + 1 < TICKS:
                inputs = jnp.concatenate([embeds[tick_index][None], outputs[:-1]], axis=0)
        cotangent = cot_rows
        backward_outs = []
        part_first = jnp.zeros((SECTIONS, D, FF), jnp.float32)
        part_second = jnp.zeros((SECTIONS, D, FF), jnp.float32)
        for tick_index in range(TICKS):
            tick_lengths = group_lengths[tick_index + sections]
            grads_in, term_first, term_second = lax.map(backward_item, (saved_inputs[:, tick_index], cotangent, w_first, w_second_t, tick_lengths))
            part_first = part_first + term_first
            part_second = part_second + term_second
            backward_outs.append(grads_in)
            if tick_index + 1 < TICKS:
                cotangent = jnp.concatenate([grads_in[1:], losses[tick_index][None]], axis=0)
        rounded_first = lax.optimization_barrier(part_first.astype(jnp.bfloat16)).astype(jnp.float32)
        rounded_second = lax.optimization_barrier(part_second.astype(jnp.bfloat16)).astype(jnp.float32)
        new_carry = (sums_carry[0] + rounded_first, sums_carry[1] + rounded_second)
        return (new_carry, (jnp.stack(forward_outs, axis=1), jnp.stack(backward_outs, axis=1)))
    start_carry = (jnp.zeros((SECTIONS, D, FF), jnp.float32), jnp.zeros((SECTIONS, D, FF), jnp.float32))
    sums_final, leaving = lax.scan(one_group, start_carry, (lengths, act_arrive, embed_next, cot_arrive, loss_cot, stash))
    step_first = adam_step(sums_final[0], m_first, v_first)
    step_second = adam_step(sums_final[1], m_second, v_second)
    return (leaving[0], leaving[1], step_first, step_second)
```

```python
import functools

import jax
import jax.numpy as jnp
from jax import lax
from jax.experimental import pallas as pl
from jax.experimental.pallas import tpu as pltpu
from jax.sharding import PartitionSpec as P


D = 512
FF = 2048
ROWS = 256
TICKS = 3
CHUNK = 512
NORM_EPS = 1e-05
ADAM_EPS = 1e-08
BETA_ONE = 0.9
BETA_TWO = 0.98
CORRECT_ONE = 1.0 - 0.9**10
CORRECT_TWO = 1.0 - 0.98**10
GELU = 0.7978845608
CUBIC = 0.044715
ALPHA = 1500.0**0.25
F32 = jnp.float32
BF16 = jnp.bfloat16

VMEM = pl.BlockSpec(memory_space=pltpu.VMEM)
SMEM = pl.BlockSpec(memory_space=pltpu.SMEM)


def call(kernel, outs, *args, scratch=(), smem=0, flops=0, limit=None):
    return pl.pallas_call(
        kernel,
        out_shape=[jax.ShapeDtypeStruct(s, d) for s, d in outs],
        in_specs=[SMEM] * smem + [VMEM] * (len(args) - smem),
        out_specs=[VMEM] * len(outs),
        scratch_shapes=list(scratch),
        cost_estimate=pl.CostEstimate(flops=flops, transcendentals=0, bytes_accessed=0),
        compiler_params=pltpu.CompilerParams(vmem_limit_bytes=limit or (16 << 20)),
    )(*args)


def dot(a, b):
    return jnp.dot(a, b, preferred_element_type=F32)


def dot_t(a, b):
    return lax.dot_general(a, b, (((1,), (1,)), ((), ())), preferred_element_type=F32)


def chunks():
    return [slice(c, c + CHUNK) for c in range(0, FF, CHUNK)]


def gelu_only(pre):
    u = pre * pre
    t = jnp.tanh(pre * (GELU + (GELU * CUBIC) * u))
    half = 0.5 * pre
    return half + half * t


def gelu_both(pre):
    u = pre * pre
    t = jnp.tanh(pre * (GELU + (GELU * CUBIC) * u))
    half = 0.5 * pre
    value = half + half * t
    slope = (0.5 + 0.5 * t) + (half - half * (t * t)) * (GELU + (3.0 * GELU * CUBIC) * u)
    return value, slope


def live(length):
    return lax.broadcasted_iota(jnp.int32, (ROWS, 1), 0) < length


def norm_parts(summed, length):
    center = summed - jnp.mean(summed, axis=1, keepdims=True)
    inv = lax.rsqrt(jnp.mean(center * center, axis=1, keepdims=True) + NORM_EPS)
    return center * inv, jnp.where(live(length), inv, 0.0), inv


def forward_tick(x, w1, w2, length):
    acc = ALPHA * x.astype(F32)
    for c in chunks():
        h = gelu_only(dot(x, w1[:, c])).astype(BF16)
        acc = acc + dot_t(h, w2[:, c])
    center = acc - jnp.mean(acc, axis=1, keepdims=True)
    inv = lax.rsqrt(jnp.mean(center * center, axis=1, keepdims=True) + NORM_EPS)
    return jnp.where(live(length), center * inv, 0.0).astype(BF16)


def grad_of_sum(cot, normed, inv_live):
    g = cot.astype(F32)
    mean_g = jnp.mean(g, axis=1, keepdims=True)
    mean_gn = jnp.mean(g * normed, axis=1, keepdims=True)
    return inv_live * (g - mean_g - normed * mean_gn)


def back_zero_kernel(lens, ids, w1, w2, stash, cot, gin, gp, h, gs, slope):
    length = lens[ids[1], ids[0]]
    x = stash[0, 0, 0]
    acc = ALPHA * x.astype(F32)
    for c in chunks():
        value, s = gelu_both(dot(x, w1[0, :, c]))
        value = value.astype(BF16)
        h[:, c] = value
        slope[:, c] = s
        acc = acc + dot_t(value, w2[0, :, c])
    normed, inv_live, _ = norm_parts(acc, length)
    total = grad_of_sum(cot[0, 0], normed, inv_live)
    total_b = total.astype(BF16)
    gs[...] = total_b
    acc = ALPHA * total
    for c in chunks():
        g = (dot(total_b, w2[0, :, c]) * slope[:, c]).astype(BF16)
        gp[:, c] = g
        acc = acc + dot_t(g, w1[0, :, c])
    gin[...] = acc.astype(BF16)


def prepare_kernel(lens, ids, w1, w2, stash, h, slope, normed, inv):
    for k in (1, 2):
        length = lens[ids[1], ids[0] + k]
        x = stash[0, 0, k]
        acc = ALPHA * x.astype(F32)
        for c in chunks():
            value, s = gelu_both(dot(x, w1[0, :, c]))
            value = value.astype(BF16)
            h[k - 1, :, c] = value
            slope[k - 1, :, c] = s
            acc = acc + dot_t(value, w2[0, :, c])
        nrm, inv_live, _ = norm_parts(acc, length)
        normed[k - 1] = nrm
        inv[k - 1] = jnp.broadcast_to(inv_live, (ROWS, 128))


def back_one_kernel(ids, w1, w2, passed, loss, slope, normed, inv, gin, gp, gs):
    cot = jnp.where(ids[0] == ids[2], loss[0, 0], passed[...])
    total = grad_of_sum(cot, normed[0], inv[0][:, :1])
    total_b = total.astype(BF16)
    gs[...] = total_b
    acc = ALPHA * total
    for c in chunks():
        g = (dot(total_b, w2[0, :, c]) * slope[0, :, c]).astype(BF16)
        gp[:, c] = g
        acc = acc + dot_t(g, w1[0, :, c])
    gin[...] = acc.astype(BF16)


def owner_rows(ref, ids):
    group = ids[1]
    chip, core = group // 2, group % 2
    parts = []
    for which in (core, 1 - core):
        for j in range(4):
            block = 2 * ((chip + j) % 4) + which
            parts.append(ref[pl.ds(pl.multiple_of(block * 64, 64), 64), :])
    return jnp.concatenate(parts, axis=0)


def terms_kernel(ids, stash, gp0, gp1, gs0, gs1, h0, h12, first, second, x_rows, left):
    for i, a in enumerate((stash[0, 0, 0], stash[0, 0, 1], gs0[...], gs1[...], stash[0, 0, 2])):
        left[i] = jnp.transpose(a)
    a0, a1 = owner_rows(left.at[0], ids), owner_rows(left.at[1], ids)
    for c in chunks():
        first[:, c] = dot(a0, gp0[:, c]) + dot(a1, gp1[:, c])
    a0, a1 = owner_rows(left.at[2], ids), owner_rows(left.at[3], ids)
    for c in chunks():
        second[:, c] = dot(a0, h0[:, c]) + dot(a1, h12[0, :, c])
    x_rows[...] = owner_rows(left.at[4], ids)


def back_two_kernel(ids, passed, loss, normed, inv, h12, second, total_out, keep, send, left):
    cot = jnp.where(ids[0] == ids[2], loss[0, 1], passed[...])
    total = grad_of_sum(cot, normed[1], inv[1][:, :1])
    total_out[...] = total
    left[...] = jnp.transpose(total.astype(BF16))
    a = owner_rows(left, ids)
    for c in chunks():
        r = second[:, c] + dot(a, h12[1, :, c])
        keep[:, c] = r[:256]
        send[:, c] = r[256:].astype(BF16)


def back_two_first_kernel(w2, total, slope, x_rows, first, gp, keep, send):
    total_b = total[...].astype(BF16)
    a = x_rows[...]
    for c in chunks():
        g = (dot(total_b, w2[0, :, c]) * slope[1, :, c]).astype(BF16)
        gp[:, c] = g
        r = first[:, c] + dot(a, g)
        keep[:, c] = r[:256]
        send[:, c] = r[256:].astype(BF16)


def back_leave_kernel(w1, total, gp, gin0, gin1, leave):
    leave[0, 0, 0] = gin0[...]
    leave[0, 0, 1] = gin1[...]
    acc = ALPHA * total[...]
    for c in chunks():
        acc = acc + dot_t(gp[:, c], w1[0, :, c])
    leave[0, 0, 2] = acc.astype(BF16)


def forward_zero_kernel(lens, ids, w1, w2, x, out):
    out[...] = forward_tick(x[0, 0], w1[0], w2[0], lens[ids[1], ids[2] - ids[0]])


def forward_one_kernel(lens, ids, w1, w2, passed, embed, out):
    x = jnp.where(ids[0] == 0, embed[0, 0], passed[...])
    out[...] = forward_tick(x, w1[0], w2[0], lens[ids[1], ids[2] - ids[0] + 1])


def forward_two_kernel(lens, ids, w1, w2, passed, embed, out0, out1, leave):
    leave[0, 0, 0] = out0[...]
    leave[0, 0, 1] = out1[...]
    x = jnp.where(ids[0] == 0, embed[0, 1], passed[...])
    leave[0, 0, 2] = forward_tick(x, w1[0], w2[0], lens[ids[1], ids[2] - ids[0] + 2])


def ring_start_kernel(keep, got, up, down, mine, later):
    s = [keep[64 * j : 64 * j + 64] + got[64 * j : 64 * j + 64].astype(F32) for j in range(4)]
    up[:32] = s[2][:32].astype(BF16)
    up[32:] = s[1][32:].astype(BF16)
    down[:32] = s[2][32:].astype(BF16)
    down[32:] = s[3][:32].astype(BF16)
    mine[...] = s[0]
    later[:32] = s[1][:32]
    later[32:] = s[3][32:]


def ring_next_kernel(mine, later, got_up, got_down, up, down, part):
    up[...] = (later[:32] + got_up[:32].astype(F32)).astype(BF16)
    down[...] = (later[32:] + got_down[:32].astype(F32)).astype(BF16)
    part[:32] = mine[:32] + got_down[32:].astype(F32)
    part[32:] = mine[32:] + got_up[32:].astype(F32)


def adam_kernel(part, got_up, got_down, m, v, step):
    for rows, got in ((slice(0, 32), got_up), (slice(32, 64), got_down)):
        g = part[rows] + got[...].astype(F32)
        m_new = BETA_ONE * m[0, rows] + (1.0 - BETA_ONE) * g
        v_new = BETA_TWO * v[0, rows] + (1.0 - BETA_TWO) * g * g
        step[0, rows] = m_new / CORRECT_ONE / (jnp.sqrt(v_new / CORRECT_TWO) + ADAM_EPS)


def shifted(x, by):
    size = lax.axis_size("section")
    return lax.ppermute(x, "section", [(i, i + by) for i in range(size) if 0 <= i + by < size])


def along_x(x, by):
    return lax.ppermute(x, "dp", [(i, ((i // 2 + by) % 4) * 2 + i % 2) for i in range(8)])


def other_core(x):
    return lax.ppermute(x, "dp", [(i, i ^ 1) for i in range(8)])


def tie(*xs):
    return lax.optimization_barrier(xs)


def on_device(
    w1, w2, m_first, v_first, m_second, v_second, lens, act, cot, embed, loss, stash
):
    section = lax.axis_index("section")
    group = lax.axis_index("dp")
    last = lax.axis_size("section") - 1
    ids = jnp.stack([section, group, jnp.int32(last)])
    mm = 2 * ROWS * D * FF
    small, wide = (ROWS, D), (ROWS, FF)

    gin0, gp0, h0, gs0 = call(
        back_zero_kernel, [(small, BF16), (wide, BF16), (wide, BF16), (small, BF16)],
        lens, ids, w1, w2, stash, cot, smem=2, flops=4 * mm,
        scratch=[pltpu.VMEM(wide, F32)],
    )
    back1 = shifted(gin0, -1)
    act, gin0 = tie(act, gin0)
    (out0,) = call(
        forward_zero_kernel, [(small, BF16)], lens, ids, w1, w2, act, smem=2, flops=2 * mm
    )
    ahead1 = shifted(out0, 1)
    stash2, out0 = tie(stash, out0)
    h12, slope12, normed12, inv12 = call(
        prepare_kernel,
        [((2, ROWS, FF), BF16), ((2, ROWS, FF), F32), ((2, ROWS, D), F32), ((2, ROWS, 128), F32)],
        lens, ids, w1, w2, stash2, smem=2, flops=4 * mm,
    )
    gin1, gp1, gs1 = call(
        back_one_kernel, [(small, BF16), (wide, BF16), (small, BF16)],
        ids, w1, w2, back1, loss, slope12, normed12, inv12, smem=1, flops=2 * mm,
    )
    back2 = shifted(gin1, -1)
    acc_first, acc_second, x_rows = call(
        terms_kernel, [((D, FF), F32), ((D, FF), F32), ((D, ROWS), BF16)],
        ids, stash2, gp0, gp1, gs0, gs1, h0, h12, smem=1, flops=4 * mm,
        scratch=[pltpu.VMEM((5, D, ROWS), BF16)],
    )
    (out1,) = call(
        forward_one_kernel, [(small, BF16)], lens, ids, w1, w2, ahead1, embed,
        smem=2, flops=2 * mm,
    )
    ahead2 = shifted(out1, 1)
    total2, keep_second, send_second = call(
        back_two_kernel, [(small, F32), ((256, FF), F32), ((256, FF), BF16)],
        ids, back2, loss, normed12, inv12, h12, acc_second, smem=1, flops=mm,
        scratch=[pltpu.VMEM((D, ROWS), BF16)],
    )
    got_second = other_core(send_second)
    gp2, keep_first, send_first = call(
        back_two_first_kernel, [(wide, BF16), ((256, FF), F32), ((256, FF), BF16)],
        w2, total2, slope12, x_rows, acc_first, flops=2 * mm,
    )
    got_first = other_core(send_first)

    def ring_start(keep, got):
        return call(
            ring_start_kernel,
            [((64, FF), BF16), ((64, FF), BF16), ((64, FF), F32), ((64, FF), F32)], keep, got,
        )

    def ring_next(mine, later, got_up, got_down):
        return call(
            ring_next_kernel, [((32, FF), BF16), ((32, FF), BF16), ((64, FF), F32)],
            mine, later, got_up, got_down,
        )

    def adam(part, got_up, got_down, m, v):
        return call(adam_kernel, [((1, 64, FF), F32)], part, got_up, got_down, m, v)[0]

    up_s, down_s, mine_s, later_s = ring_start(keep_second, got_second)
    up_s, down_s = along_x(up_s, 1), along_x(down_s, -1)
    up_f, down_f, mine_f, later_f = ring_start(keep_first, got_first)
    up_f, down_f = along_x(up_f, 1), along_x(down_f, -1)
    (cot_leave,) = call(
        back_leave_kernel, [((1, 1, 3) + small, BF16)], w1, total2, gp2, gin0, gin1, flops=mm
    )
    (act_leave,) = call(
        forward_two_kernel, [((1, 1, 3) + small, BF16)],
        lens, ids, w1, w2, ahead2, embed, out0, out1, smem=2, flops=2 * mm,
    )
    up_s, down_s, part_s = ring_next(mine_s, later_s, up_s, down_s)
    up_s, down_s = along_x(up_s, 1), along_x(down_s, -1)
    up_f, down_f, part_f = ring_next(mine_f, later_f, up_f, down_f)
    up_f, down_f = along_x(up_f, 1), along_x(down_f, -1)
    step_second = adam(part_s, up_s, down_s, m_second, v_second)
    step_first = adam(part_f, up_f, down_f, m_first, v_first)
    return (act_leave, cot_leave, step_first, step_second)


def solution(mesh):
    by_section = P("section", None, None)
    by_rows = P("section", "dp", None)
    by_group = P("dp", "section", None, None)
    ticks = P("dp", "section", None, None, None)
    every = P("dp", None, None, None)
    return jax.shard_map(
        on_device,
        mesh=mesh,
        in_specs=(by_section, by_section, by_rows, by_rows, by_rows, by_rows, P(),
                  by_group, by_group, every, every, ticks),
        out_specs=(ticks, ticks, by_rows, by_rows),
        check_vma=False,
    )
```

```python
import jax
import jax.numpy as jnp
from jax import lax
from jax.experimental import pallas as pl
from jax.experimental.pallas import tpu as pltpu
from jax.sharding import PartitionSpec as P


D = 512
FF = 2048
ROWS = 256
CHUNK = 512
NORM_EPS = 1e-05
ADAM_EPS = 1e-08
BETA_ONE = 0.9
BETA_TWO = 0.98
CORRECT_ONE = 1.0 - 0.9**10
CORRECT_TWO = 1.0 - 0.98**10
GELU = 0.7978845608
CUBIC = 0.044715
ALPHA = 1500.0**0.25
F32 = jnp.float32
BF16 = jnp.bfloat16

VMEM = pl.BlockSpec(memory_space=pltpu.VMEM)
HBM = pl.BlockSpec(memory_space=pltpu.HBM)


def call(kernel, outs, *args, scratch=(), raw=(), out=VMEM, flops=0, limit=None):
    kernel_call = pl.pallas_call(
        kernel,
        out_shape=[jax.ShapeDtypeStruct(s, d) for s, d in outs],
        in_specs=[HBM if i in raw else VMEM for i in range(len(args))],
        out_specs=[out] * len(outs),
        scratch_shapes=list(scratch),
        cost_estimate=pl.CostEstimate(flops=flops, transcendentals=0, bytes_accessed=0),
        compiler_params=pltpu.CompilerParams(vmem_limit_bytes=limit or (16 << 20)),
    )
    args = [
        pltpu.with_memory_space_constraint(a, pltpu.HBM) if i in raw else a
        for i, a in enumerate(args)
    ]
    return kernel_call(*args)


def dot(a, b):
    return jnp.dot(a, b, preferred_element_type=F32)


def dot_t(a, b):
    return lax.dot_general(a, b, (((1,), (1,)), ((), ())), preferred_element_type=F32)


def chunks():
    return [slice(c, c + CHUNK) for c in range(0, FF, CHUNK)]


def gelu_both(pre):
    w = GELU + (GELU * CUBIC) * (pre * pre)
    a = 0.5 + 0.5 * jnp.tanh(pre * w)
    value = pre * a
    return value, a + value * (1.0 - a) * (6.0 * w - 4.0 * GELU)


def live(length):
    return lax.broadcasted_iota(jnp.int32, (ROWS, 128), 0) < length


def norm_parts(summed):
    center = summed - jnp.mean(summed, axis=1, keepdims=True)
    inv = lax.rsqrt(jnp.mean(center * center, axis=1, keepdims=True) + NORM_EPS)
    return center * inv, inv


def forward_tick(x, w1, w2, mask):
    acc = ALPHA * x.astype(F32)
    for c in chunks():
        h = gelu_both(dot(x, w1[0, :, c]))[0].astype(BF16)
        acc = acc + dot_t(h, w2[0, :, c])
    return jnp.where(mask()[:, :1] > 0.0, norm_parts(acc)[0], 0.0).astype(BF16)


def grad_of_sum(cot, normed, inv_live):
    g = cot.astype(F32)
    mean_g = jnp.mean(g, axis=1, keepdims=True)
    mean_gn = jnp.mean(g * normed, axis=1, keepdims=True)
    return inv_live * (g - mean_g - normed * mean_gn)


def back_zero_kernel(lens_hbm, w1_hbm, w2_hbm, stash_hbm, cot_hbm,
                     gin, gp, h, gs, w1, w2, x, slope, cot, lens, sem, w_sem):
    group, section = lax.axis_index("dp"), lax.axis_index("section")
    get_x = pltpu.make_async_copy(stash_hbm.at[0, 0, 0], x, sem.at[0])
    get_x.start()
    streams = [
        [
            pltpu.make_async_copy(src.at[0, :, c], dst.at[0, :, c], w_sem.at[j, i])
            for j, (src, dst) in enumerate(((w1_hbm, w1), (w2_hbm, w2)))
        ]
        for i, c in enumerate(chunks())
    ]
    get_lens = pltpu.make_async_copy(lens_hbm, lens, sem.at[1])
    get_cot = pltpu.make_async_copy(cot_hbm.at[0, 0], cot, sem.at[2])
    for pair in streams[:2]:
        for copy in pair:
            copy.start()
    get_lens.start()
    get_x.wait()
    acc = ALPHA * x[...].astype(F32)
    for i, c in enumerate(chunks()):
        get_w1, get_w2 = streams[i]
        get_w1.wait()
        if i + 2 < len(streams):
            streams[i + 2][0].start()
        if i == 1:
            get_cot.start()
        value, s = gelu_both(dot(x[...], w1[0, :, c]))
        value = value.astype(BF16)
        h[:, c] = value
        slope[:, c] = s
        get_w2.wait()
        if i + 2 < len(streams):
            streams[i + 2][1].start()
        acc = acc + dot_t(value, w2[0, :, c])
    normed, inv = norm_parts(acc)
    get_lens.wait()
    get_cot.wait()
    inv = jnp.where(live(lens[group, section])[:, :1], inv, 0.0)
    total = grad_of_sum(cot[...], normed, inv)
    total_b = total.astype(BF16)
    gs[...] = total_b
    acc = ALPHA * total
    for c in chunks():
        g = (dot(total_b, w2[0, :, c]) * slope[:, c]).astype(BF16)
        gp[:, c] = g
        acc = acc + dot_t(g, w1[0, :, c])
    gin[...] = acc.astype(BF16)


def prepare(k, w1, w2, stash, masks, h, slope, normed, inv):
    x = stash[0, 0, k]
    acc = ALPHA * x.astype(F32)
    for c in chunks():
        value, s = gelu_both(dot(x, w1[0, :, c]))
        value = value.astype(BF16)
        h[:, c] = value
        slope[:, c] = s
        acc = acc + dot_t(value, w2[0, :, c])
    nrm, inv_std = norm_parts(acc)
    normed[...] = nrm
    inv[...] = masks[k - 1] * inv_std


def prepare_one_kernel(*refs):
    prepare(1, *refs)


def prepare_two_kernel(*refs):
    prepare(2, *refs)


def back_one_kernel(w1, w2, passed, loss, slope, normed, inv, gin, gp, gs):
    cot = jnp.where(at_end(), loss[0, 0], passed[...])
    total = grad_of_sum(cot, normed[...], inv[:, :1])
    total_b = total.astype(BF16)
    gs[...] = total_b
    acc = ALPHA * total
    for c in chunks():
        g = (dot(total_b, w2[0, :, c]) * slope[:, c]).astype(BF16)
        gp[:, c] = g
        acc = acc + dot_t(g, w1[0, :, c])
    gin[...] = acc.astype(BF16)


def at_end():
    return lax.axis_index("section") == lax.axis_size("section") - 1


def owner_rows(ref):
    group = lax.axis_index("dp")
    chip, core = group // 2, group % 2
    parts = []
    for which in (core, 1 - core):
        for j in range(4):
            block = 2 * ((chip + j) % 4) + which
            parts.append(ref[pl.ds(pl.multiple_of(block * 64, 64), 64), :])
    return jnp.concatenate(parts, axis=0)


def terms_kernel(stash, gp0, gp1, gs0, gs1, h0, h1, first, second, x_rows, left):
    for i, a in enumerate((stash[0, 0, 0], stash[0, 0, 1], gs0[...], gs1[...], stash[0, 0, 2])):
        left[i] = jnp.transpose(a)
    a0, a1 = owner_rows(left.at[0]), owner_rows(left.at[1])
    for c in chunks():
        first[:, c] = dot(a0, gp0[:, c]) + dot(a1, gp1[:, c])
    a0, a1 = owner_rows(left.at[2]), owner_rows(left.at[3])
    for c in chunks():
        second[:, c] = dot(a0, h0[:, c]) + dot(a1, h1[:, c])
    x_rows[...] = owner_rows(left.at[4])


def back_two_kernel(passed, loss, normed, inv, h2, second, total_out, keep, send, left):
    cot = jnp.where(at_end(), loss[0, 1], passed[...])
    total = grad_of_sum(cot, normed[...], inv[:, :1])
    total_out[...] = total
    left[...] = jnp.transpose(total.astype(BF16))
    a = owner_rows(left)
    for c in chunks():
        r = second[:, c] + dot(a, h2[:, c])
        keep[:, c] = r[:256]
        send[:, c] = r[256:].astype(BF16)


def back_two_first_kernel(w2, total, slope, x_rows, first, gp, keep, send):
    total_b = total[...].astype(BF16)
    a = x_rows[...]
    for c in chunks():
        g = (dot(total_b, w2[0, :, c]) * slope[:, c]).astype(BF16)
        gp[:, c] = g
        r = first[:, c] + dot(a, g)
        keep[:, c] = r[:256]
        send[:, c] = r[256:].astype(BF16)


def leaving(leave, early, last, sem):
    copies = [
        pltpu.make_async_copy(src, leave.at[0, 0, k], sem.at[k])
        for k, src in enumerate(early + (last,))
    ]
    copies[0].start()
    copies[1].start()

    def finish():
        copies[2].start()
        for copy in copies:
            copy.wait()

    return finish


def back_leave_kernel(w1, total, gp, gin0, gin1, leave, gin2, sem):
    finish = leaving(leave, (gin0, gin1), gin2, sem)
    acc = ALPHA * total[...]
    for c in chunks():
        acc = acc + dot_t(gp[:, c], w1[0, :, c])
    gin2[...] = acc.astype(BF16)
    finish()


def forward_zero_kernel(lens_hbm, w1, w2, act, out, back_masks, masks, lens, sem):
    get_lens = pltpu.make_async_copy(lens_hbm, lens, sem)
    get_lens.start()
    group, section = lax.axis_index("dp"), lax.axis_index("section")
    last = lax.axis_size("section") - 1

    def mask():
        get_lens.wait()
        for k in (1, 2):
            back_masks[k - 1] = live(lens[group, section + k]).astype(F32)
            masks[k - 1] = live(lens[group, last - section + k]).astype(F32)
        return live(lens[group, last - section]).astype(F32)

    out[...] = forward_tick(act[0, 0], w1, w2, mask)


def forward_one_kernel(w1, w2, passed, embed, masks, out):
    x = jnp.where(lax.axis_index("section") == 0, embed[0, 0], passed[...])
    out[...] = forward_tick(x, w1, w2, lambda: masks[0])


def forward_two_kernel(w1, w2, passed, embed, masks, out0, out1, leave, out2, sem):
    finish = leaving(leave, (out0, out1), out2, sem)
    x = jnp.where(lax.axis_index("section") == 0, embed[0, 1], passed[...])
    out2[...] = forward_tick(x, w1, w2, lambda: masks[1])
    finish()


def ring_start_kernel(keep, got, up, down, mine, later):
    s = [keep[64 * j : 64 * j + 64] + got[64 * j : 64 * j + 64].astype(F32) for j in range(4)]
    up[:32] = s[2][:32].astype(BF16)
    up[32:] = s[1][32:].astype(BF16)
    down[:32] = s[2][32:].astype(BF16)
    down[32:] = s[3][:32].astype(BF16)
    mine[...] = s[0]
    later[:32] = s[1][:32]
    later[32:] = s[3][32:]


def ring_next_kernel(mine, later, got_up, got_down, up, down, part):
    up[...] = (later[:32] + got_up[:32].astype(F32)).astype(BF16)
    down[...] = (later[32:] + got_down[:32].astype(F32)).astype(BF16)
    part[:32] = mine[:32] + got_down[32:].astype(F32)
    part[32:] = mine[32:] + got_up[32:].astype(F32)


def adam_kernel(part, got_up, got_down, m, v, step, new, sem):
    copies = []
    for i in range(4):
        rows, got_rows = slice(16 * i, 16 * i + 16), slice(16 * (i % 2), 16 * (i % 2) + 16)
        g = part[rows] + (got_up, got_down)[i // 2][got_rows].astype(F32)
        m_new = BETA_ONE * m[0, rows] + (1.0 - BETA_ONE) * g
        v_new = BETA_TWO * v[0, rows] + (1.0 - BETA_TWO) * g * g
        new[rows] = m_new / CORRECT_ONE / (jnp.sqrt(v_new / CORRECT_TWO) + ADAM_EPS)
        copies.append(pltpu.make_async_copy(new.at[rows], step.at[0, rows], sem.at[i]))
        copies[i].start()
    for copy in copies:
        copy.wait()


def shifted(x, by):
    size = lax.axis_size("section")
    return lax.ppermute(x, "section", [(i, (i + by) % size) for i in range(size)])


def along_x(x, by):
    return lax.ppermute(x, "dp", [(i, ((i // 2 + by) % 4) * 2 + i % 2) for i in range(8)])


def other_core(x):
    return lax.ppermute(x, "dp", [(i, i ^ 1) for i in range(8)])


def window(
    w1, w2, m_first, v_first, m_second, v_second, lens, act, cot, embed, loss, stash
):
    mm = 2 * ROWS * D * FF
    small, wide, masks2 = (ROWS, D), (ROWS, FF), (2, ROWS, 128)
    lens_scratch = [pltpu.SMEM(lens.shape, jnp.int32)]

    gin0, gp0, h0, gs0, w1, w2 = call(
        back_zero_kernel,
        [(small, BF16), (wide, BF16), (wide, BF16), (small, BF16), (w1.shape, BF16), (w2.shape, BF16)],
        lens, w1, w2, stash, cot, raw=range(5), flops=4 * mm,
        scratch=[pltpu.VMEM(small, BF16), pltpu.VMEM(wide, F32), pltpu.VMEM(small, BF16)]
        + lens_scratch + [pltpu.SemaphoreType.DMA((3,)), pltpu.SemaphoreType.DMA((2, 4))],
    )
    back1 = shifted(gin0, -1)
    out0, back_masks, masks = call(
        forward_zero_kernel, [(small, BF16), (masks2, F32), (masks2, F32)], lens, w1, w2, act,
        raw=(0,), flops=2 * mm, scratch=lens_scratch + [pltpu.SemaphoreType.DMA],
    )
    ahead1 = shifted(out0, 1)

    def prepared(kernel):
        return call(
            kernel, [(wide, BF16), (wide, F32), (small, F32), ((ROWS, 128), F32)],
            w1, w2, stash, back_masks, flops=2 * mm,
        )

    h1, slope1, normed1, inv1 = prepared(prepare_one_kernel)
    gin1, gp1, gs1 = call(
        back_one_kernel, [(small, BF16), (wide, BF16), (small, BF16)],
        w1, w2, back1, loss, slope1, normed1, inv1, flops=2 * mm,
    )
    back2 = shifted(gin1, -1)
    h2, slope2, normed2, inv2 = prepared(prepare_two_kernel)
    acc_first, acc_second, x_rows = call(
        terms_kernel, [((D, FF), F32), ((D, FF), F32), ((D, ROWS), BF16)],
        stash, gp0, gp1, gs0, gs1, h0, h1, flops=4 * mm,
        scratch=[pltpu.VMEM((5, D, ROWS), BF16)],
    )
    total2, keep_second, send_second = call(
        back_two_kernel, [(small, F32), ((256, FF), F32), ((256, FF), BF16)],
        back2, loss, normed2, inv2, h2, acc_second, flops=mm,
        scratch=[pltpu.VMEM((D, ROWS), BF16)],
    )
    got_second = other_core(send_second)
    gp2, keep_first, send_first = call(
        back_two_first_kernel, [(wide, BF16), ((256, FF), F32), ((256, FF), BF16)],
        w2, total2, slope2, x_rows, acc_first, flops=2 * mm,
    )
    got_first = other_core(send_first)
    (out1,) = call(
        forward_one_kernel, [(small, BF16)], w1, w2, ahead1, embed, masks, flops=2 * mm
    )
    ahead2 = shifted(out1, 1)

    def ring_start(keep, got):
        return call(
            ring_start_kernel,
            [((64, FF), BF16), ((64, FF), BF16), ((64, FF), F32), ((64, FF), F32)], keep, got,
        )

    def ring_next(mine, later, got_up, got_down):
        return call(
            ring_next_kernel, [((32, FF), BF16), ((32, FF), BF16), ((64, FF), F32)],
            mine, later, got_up, got_down,
        )

    def adam(part, got_up, got_down, m, v):
        return call(
            adam_kernel, [((1, 64, FF), F32)], part, got_up, got_down, m, v, out=HBM,
            scratch=[pltpu.VMEM((64, FF), F32), pltpu.SemaphoreType.DMA((4,))],
        )[0]

    def both_ways(up, down):
        up = along_x(up, 1)
        down = along_x(down, -1)
        return up, down

    out_scratch = [pltpu.VMEM(small, BF16), pltpu.SemaphoreType.DMA((3,))]
    up_s, down_s, mine_s, later_s = ring_start(keep_second, got_second)
    up_s, down_s = both_ways(up_s, down_s)
    up_f, down_f, mine_f, later_f = ring_start(keep_first, got_first)
    up_f, down_f = both_ways(up_f, down_f)
    up_s, down_s, part_s = ring_next(mine_s, later_s, up_s, down_s)
    up_s, down_s = both_ways(up_s, down_s)
    (cot_leave,) = call(
        back_leave_kernel, [((1, 1, 3) + small, BF16)], w1, total2, gp2, gin0, gin1,
        out=HBM, flops=mm, scratch=out_scratch,
    )
    up_f, down_f, part_f = ring_next(mine_f, later_f, up_f, down_f)
    up_f, down_f = both_ways(up_f, down_f)
    (act_leave,) = call(
        forward_two_kernel, [((1, 1, 3) + small, BF16)], w1, w2, ahead2, embed, masks, out0, out1,
        out=HBM, flops=2 * mm, scratch=out_scratch,
    )
    step_second = adam(part_s, up_s, down_s, m_second, v_second)
    step_first = adam(part_f, up_f, down_f, m_first, v_first)
    return (act_leave, cot_leave, step_first, step_second)


def solution(mesh):
    by_section = P("section", None, None)
    by_rows = P("section", "dp", None)
    by_group = P("dp", "section", None, None)
    ticks = P("dp", "section", None, None, None)
    every = P("dp", None, None, None)
    return jax.shard_map(
        window,
        mesh=mesh,
        in_specs=(by_section, by_section, by_rows, by_rows, by_rows, by_rows, P(),
                  by_group, by_group, every, every, ticks),
        out_specs=(ticks, ticks, by_rows, by_rows),
        check_vma=False,
    )
```

```python
import jax
import jax.numpy as jnp
from jax import lax
from jax.experimental import pallas as pl
from jax.experimental.pallas import tpu as pltpu
from jax.sharding import PartitionSpec as P


D = 512
FF = 2048
ROWS = 256
CHUNK = 512
NORM_EPS = 1e-05
ADAM_EPS = 1e-08
BETA_ONE = 0.9
BETA_TWO = 0.98
CORRECT_ONE = 1.0 - 0.9**10
CORRECT_TWO = 1.0 - 0.98**10
GELU = 0.7978845608
CUBIC = 0.044715
ALPHA = 1500.0**0.25
F32 = jnp.float32
BF16 = jnp.bfloat16

VMEM = pl.BlockSpec(memory_space=pltpu.VMEM)
HBM = pl.BlockSpec(memory_space=pltpu.HBM)


def call(kernel, outs, *args, scratch=(), raw=(), out=VMEM, flops=0, limit=None):
    kernel_call = pl.pallas_call(
        kernel,
        out_shape=[jax.ShapeDtypeStruct(s, d) for s, d in outs],
        in_specs=[HBM if i in raw else VMEM for i in range(len(args))],
        out_specs=[out] * len(outs),
        scratch_shapes=list(scratch),
        cost_estimate=pl.CostEstimate(flops=flops, transcendentals=0, bytes_accessed=0),
        compiler_params=pltpu.CompilerParams(vmem_limit_bytes=limit or (16 << 20)),
    )
    args = [
        pltpu.with_memory_space_constraint(a, pltpu.HBM) if i in raw else a
        for i, a in enumerate(args)
    ]
    return kernel_call(*args)


def dot(a, b):
    return jnp.dot(a, b, preferred_element_type=F32)


def dot_t(a, b):
    return lax.dot_general(a, b, (((1,), (1,)), ((), ())), preferred_element_type=F32)


def chunks(size=CHUNK):
    return [slice(c, c + size) for c in range(0, FF, size)]


def gelu_both(pre):
    w = GELU + (GELU * CUBIC) * (pre * pre)
    a = 0.5 + 0.5 * jnp.tanh(pre * w)
    value = pre * a
    return value, a + value * (1.0 - a) * (6.0 * w - 4.0 * GELU)


def live(length):
    return lax.broadcasted_iota(jnp.int32, (ROWS, 128), 0) < length


def norm_parts(summed):
    center = summed - jnp.mean(summed, axis=1, keepdims=True)
    inv = lax.rsqrt(jnp.mean(center * center, axis=1, keepdims=True) + NORM_EPS)
    return center * inv, inv


def forward_tick(x, w1, w2, mask):
    acc = ALPHA * x.astype(F32)
    columns = chunks(256)
    pre = dot(x, w1[0, :, columns[0]])
    for i, c in enumerate(columns):
        ahead = dot(x, w1[0, :, columns[i + 1]]) if i + 1 < len(columns) else None
        h = gelu_both(pre)[0].astype(BF16)
        acc = acc + dot_t(h, w2[0, :, c])
        pre = ahead
    return jnp.where(mask()[:, :1] > 0.0, norm_parts(acc)[0], 0.0).astype(BF16)


def grad_of_sum(cot, normed, inv_live):
    g = cot.astype(F32)
    mean_g = jnp.mean(g, axis=1, keepdims=True)
    mean_gn = jnp.mean(g * normed, axis=1, keepdims=True)
    return inv_live * (g - mean_g - normed * mean_gn)


def back_zero_kernel(lens_hbm, w1_hbm, w2_hbm, stash_hbm, cot_hbm,
                     gin, gp, h, gs, w1, w2, back_masks, masks,
                     x, slope, cot, lens, sem, w_sem):
    group, section = lax.axis_index("dp"), lax.axis_index("section")
    get_x = pltpu.make_async_copy(stash_hbm.at[0, 0, 0], x, sem.at[0])
    get_x.start()
    streams = [
        [
            pltpu.make_async_copy(src.at[0, :, c], dst.at[0, :, c], w_sem.at[j, i])
            for j, (src, dst) in enumerate(((w1_hbm, w1), (w2_hbm, w2)))
        ]
        for i, c in enumerate(chunks())
    ]
    get_lens = pltpu.make_async_copy(lens_hbm, lens, sem.at[1])
    get_cot = pltpu.make_async_copy(cot_hbm.at[0, 0], cot, sem.at[2])
    for pair in streams[:2]:
        for copy in pair:
            copy.start()
    get_lens.start()
    get_x.wait()
    acc = ALPHA * x[...].astype(F32)
    pre = None
    for i in range(len(streams) + 1):
        if i < len(streams):
            streams[i][0].wait()
            if i + 2 < len(streams):
                streams[i + 2][0].start()
        if i > 0:
            streams[i - 1][1].wait()
            if i + 1 < len(streams):
                streams[i + 1][1].start()
        if i == 1:
            get_cot.start()
        ahead = dot(x[...], w1[0, :, chunks()[i]]) if i < len(streams) else None
        if i > 0:
            c = chunks()[i - 1]
            value, s = gelu_both(pre)
            value = value.astype(BF16)
            h[:, c] = value
            slope[:, c] = s
            acc = acc + dot_t(value, w2[0, :, c])
        pre = ahead
    normed, inv = norm_parts(acc)
    get_lens.wait()
    get_cot.wait()
    inv = jnp.where(live(lens[group, section])[:, :1], inv, 0.0)
    total = grad_of_sum(cot[...], normed, inv)
    total_b = total.astype(BF16)
    gs[...] = total_b
    acc = ALPHA * total
    for c in chunks(1024):
        g = (dot(total_b, w2[0, :, c]) * slope[:, c]).astype(BF16)
        gp[:, c] = g
        acc = acc + dot_t(g, w1[0, :, c])
    gin[...] = acc.astype(BF16)
    last = lax.axis_size("section") - 1
    for k in (1, 2):
        back_masks[k - 1] = live(lens[group, section + k]).astype(F32)
    for k in range(3):
        masks[k] = live(lens[group, last - section + k]).astype(F32)


def prepare(k, w1, w2, stash, masks, h, slope, normed, inv):
    x = stash[0, 0, k]
    acc = ALPHA * x.astype(F32)
    for c in chunks(256):
        value, s = gelu_both(dot(x, w1[0, :, c]))
        value = value.astype(BF16)
        h[:, c] = value
        slope[:, c] = s
        acc = acc + dot_t(value, w2[0, :, c])
    nrm, inv_std = norm_parts(acc)
    normed[...] = nrm
    inv[...] = masks[k - 1] * inv_std


def prepare_one_kernel(*refs):
    prepare(1, *refs)


def prepare_two_kernel(*refs):
    prepare(2, *refs)


def back_one_kernel(w1, w2, passed, loss, slope, normed, inv, gin, gp, gs):
    cot = jnp.where(at_end(), loss[0, 0], passed[...])
    total = grad_of_sum(cot, normed[...], inv[:, :1])
    total_b = total.astype(BF16)
    gs[...] = total_b
    acc = ALPHA * total
    for c in chunks(1024):
        g = (dot(total_b, w2[0, :, c]) * slope[:, c]).astype(BF16)
        gp[:, c] = g
        acc = acc + dot_t(g, w1[0, :, c])
    gin[...] = acc.astype(BF16)


def at_end():
    return lax.axis_index("section") == lax.axis_size("section") - 1


def owner_rows(ref):
    group = lax.axis_index("dp")
    chip, core = group // 2, group % 2
    parts = []
    for which in (core, 1 - core):
        for j in range(4):
            block = 2 * ((chip + j) % 4) + which
            parts.append(ref[pl.ds(pl.multiple_of(block * 64, 64), 64), :])
    return jnp.concatenate(parts, axis=0)


def terms_zero_kernel(stash, gp, gs, h, first, second, x1_rows, x2_rows, left):
    for i, a in enumerate((stash[0, 0, 0], gs[...], stash[0, 0, 1], stash[0, 0, 2])):
        left[i] = jnp.transpose(a)
    a = owner_rows(left.at[0])
    for c in chunks():
        first[:, c] = dot(a, gp[:, c])
    a = owner_rows(left.at[1])
    for c in chunks():
        second[:, c] = dot(a, h[:, c])
    x1_rows[...] = owner_rows(left.at[2])
    x2_rows[...] = owner_rows(left.at[3])


def terms_one_kernel(x_rows, gp, gs, h, first0, second0, first, second, left):
    a = x_rows[...]
    for c in chunks():
        first[:, c] = first0[:, c] + dot(a, gp[:, c])
    left[...] = jnp.transpose(gs[...])
    a = owner_rows(left)
    for c in chunks():
        second[:, c] = second0[:, c] + dot(a, h[:, c])


def back_two_kernel(passed, loss, normed, inv, h2, second, total_out, keep, send, left):
    cot = jnp.where(at_end(), loss[0, 1], passed[...])
    total = grad_of_sum(cot, normed[...], inv[:, :1])
    total_out[...] = total
    left[...] = jnp.transpose(total.astype(BF16))
    a = owner_rows(left)
    for c in chunks():
        r = second[:, c] + dot(a, h2[:, c])
        keep[:, c] = r[:256]
        send[:, c] = r[256:].astype(BF16)


def back_two_first_kernel(w2, total, slope, x_rows, first, gp, keep, send):
    total_b = total[...].astype(BF16)
    a = x_rows[...]
    for c in chunks(1024):
        g = (dot(total_b, w2[0, :, c]) * slope[:, c]).astype(BF16)
        gp[:, c] = g
        r = first[:, c] + dot(a, g)
        keep[:, c] = r[:256]
        send[:, c] = r[256:].astype(BF16)


def leaving(leave, early, last, sem):
    copies = [
        pltpu.make_async_copy(src, leave.at[0, 0, k], sem.at[k])
        for k, src in enumerate(early + (last,))
    ]
    copies[0].start()
    copies[1].start()

    def finish():
        copies[2].start()
        for copy in copies:
            copy.wait()

    return finish


def back_leave_kernel(w1, total, gp, gin0, gin1, leave, gin2, sem):
    finish = leaving(leave, (gin0, gin1), gin2, sem)
    acc = ALPHA * total[...]
    for c in chunks(2048):
        acc = acc + dot_t(gp[:, c], w1[0, :, c])
    gin2[...] = acc.astype(BF16)
    finish()


def forward_zero_kernel(w1, w2, act, masks, out):
    out[...] = forward_tick(act[0, 0], w1, w2, lambda: masks[0])


def forward_one_kernel(w1, w2, passed, embed, masks, out):
    x = jnp.where(lax.axis_index("section") == 0, embed[0, 0], passed[...])
    out[...] = forward_tick(x, w1, w2, lambda: masks[1])


def forward_two_kernel(w1, w2, passed, embed, masks, out0, out1, leave, out2, sem):
    finish = leaving(leave, (out0, out1), out2, sem)
    x = jnp.where(lax.axis_index("section") == 0, embed[0, 1], passed[...])
    out2[...] = forward_tick(x, w1, w2, lambda: masks[2])
    finish()


def ring_start_kernel(keep, got, up, down, mine, later):
    s = [keep[64 * j : 64 * j + 64] + got[64 * j : 64 * j + 64].astype(F32) for j in range(4)]
    up[:32] = s[2][:32].astype(BF16)
    up[32:] = s[1][32:].astype(BF16)
    down[:32] = s[2][32:].astype(BF16)
    down[32:] = s[3][:32].astype(BF16)
    mine[...] = s[0]
    later[:32] = s[1][:32]
    later[32:] = s[3][32:]


def ring_next_kernel(mine, later, got_up, got_down, up, down, part):
    up[...] = (later[:32] + got_up[:32].astype(F32)).astype(BF16)
    down[...] = (later[32:] + got_down[:32].astype(F32)).astype(BF16)
    part[:32] = mine[:32] + got_down[32:].astype(F32)
    part[32:] = mine[32:] + got_up[32:].astype(F32)


def adam_kernel(part, got_up, got_down, m, v, step, new, sem):
    copies = []
    for i in range(4):
        rows, got_rows = slice(16 * i, 16 * i + 16), slice(16 * (i % 2), 16 * (i % 2) + 16)
        g = part[rows] + (got_up, got_down)[i // 2][got_rows].astype(F32)
        m_new = BETA_ONE * m[0, rows] + (1.0 - BETA_ONE) * g
        v_new = BETA_TWO * v[0, rows] + (1.0 - BETA_TWO) * g * g
        new[rows] = m_new / CORRECT_ONE / (jnp.sqrt(v_new / CORRECT_TWO) + ADAM_EPS)
        copies.append(pltpu.make_async_copy(new.at[rows], step.at[0, rows], sem.at[i]))
        copies[i].start()
    for copy in copies:
        copy.wait()


def shifted(x, by):
    size = lax.axis_size("section")
    return lax.ppermute(x, "section", [(i, (i + by) % size) for i in range(size)])


def along_x(x, by):
    return lax.ppermute(x, "dp", [(i, ((i // 2 + by) % 4) * 2 + i % 2) for i in range(8)])


def other_core(x):
    return lax.ppermute(x, "dp", [(i, i ^ 1) for i in range(8)])


def window(
    w1, w2, m_first, v_first, m_second, v_second, lens, act, cot, embed, loss, stash
):
    mm = 2 * ROWS * D * FF
    small, wide = (ROWS, D), (ROWS, FF)

    gin0, gp0, h0, gs0, w1, w2, back_masks, masks = call(
        back_zero_kernel,
        [(small, BF16), (wide, BF16), (wide, BF16), (small, BF16), (w1.shape, BF16), (w2.shape, BF16),
         ((2, ROWS, 128), F32), ((3, ROWS, 128), F32)],
        lens, w1, w2, stash, cot, raw=range(5), flops=4 * mm,
        scratch=[pltpu.VMEM(small, BF16), pltpu.VMEM(wide, F32), pltpu.VMEM(small, BF16)]
        + [pltpu.SMEM(lens.shape, jnp.int32), pltpu.SemaphoreType.DMA((3,)),
           pltpu.SemaphoreType.DMA((2, 4))],
    )
    back1 = shifted(gin0, -1)

    def prepared(kernel):
        return call(
            kernel, [(wide, BF16), (wide, F32), (small, F32), ((ROWS, 128), F32)],
            w1, w2, stash, back_masks, flops=2 * mm,
        )

    h1, slope1, normed1, inv1 = prepared(prepare_one_kernel)
    h2, slope2, normed2, inv2 = prepared(prepare_two_kernel)
    acc_first, acc_second, x1_rows, x2_rows = call(
        terms_zero_kernel,
        [((D, FF), F32), ((D, FF), F32), ((D, ROWS), BF16), ((D, ROWS), BF16)],
        stash, gp0, gs0, h0, flops=2 * mm, scratch=[pltpu.VMEM((4, D, ROWS), BF16)],
    )
    gin1, gp1, gs1 = call(
        back_one_kernel, [(small, BF16), (wide, BF16), (small, BF16)],
        w1, w2, back1, loss, slope1, normed1, inv1, flops=2 * mm,
    )
    back2 = shifted(gin1, -1)
    (out0,) = call(forward_zero_kernel, [(small, BF16)], w1, w2, act, masks, flops=2 * mm)
    ahead1 = shifted(out0, 1)
    acc_first, acc_second = call(
        terms_one_kernel, [((D, FF), F32), ((D, FF), F32)],
        x1_rows, gp1, gs1, h1, acc_first, acc_second, flops=2 * mm,
        scratch=[pltpu.VMEM((D, ROWS), BF16)],
    )
    total2, keep_second, send_second = call(
        back_two_kernel, [(small, F32), ((256, FF), F32), ((256, FF), BF16)],
        back2, loss, normed2, inv2, h2, acc_second, flops=mm,
        scratch=[pltpu.VMEM((D, ROWS), BF16)],
    )
    got_second = other_core(send_second)
    gp2, keep_first, send_first = call(
        back_two_first_kernel, [(wide, BF16), ((256, FF), F32), ((256, FF), BF16)],
        w2, total2, slope2, x2_rows, acc_first, flops=2 * mm,
    )
    got_first = other_core(send_first)
    (out1,) = call(
        forward_one_kernel, [(small, BF16)], w1, w2, ahead1, embed, masks, flops=2 * mm
    )
    ahead2 = shifted(out1, 1)

    def ring_start(keep, got):
        return call(
            ring_start_kernel,
            [((64, FF), BF16), ((64, FF), BF16), ((64, FF), F32), ((64, FF), F32)], keep, got,
        )

    def ring_next(mine, later, got_up, got_down):
        return call(
            ring_next_kernel, [((32, FF), BF16), ((32, FF), BF16), ((64, FF), F32)],
            mine, later, got_up, got_down,
        )

    def adam(part, got_up, got_down, m, v):
        return call(
            adam_kernel, [((1, 64, FF), F32)], part, got_up, got_down, m, v, out=HBM,
            scratch=[pltpu.VMEM((64, FF), F32), pltpu.SemaphoreType.DMA((4,))],
        )[0]

    def both_ways(up, down):
        up = along_x(up, 1)
        down = along_x(down, -1)
        return up, down

    out_scratch = [pltpu.VMEM(small, BF16), pltpu.SemaphoreType.DMA((3,))]
    up_s, down_s, mine_s, later_s = ring_start(keep_second, got_second)
    up_s, down_s = both_ways(up_s, down_s)
    up_f, down_f, mine_f, later_f = ring_start(keep_first, got_first)
    up_f, down_f = both_ways(up_f, down_f)
    up_s, down_s, part_s = ring_next(mine_s, later_s, up_s, down_s)
    up_s, down_s = both_ways(up_s, down_s)
    (cot_leave,) = call(
        back_leave_kernel, [((1, 1, 3) + small, BF16)], w1, total2, gp2, gin0, gin1,
        out=HBM, flops=mm, scratch=out_scratch,
    )
    up_f, down_f, part_f = ring_next(mine_f, later_f, up_f, down_f)
    up_f, down_f = both_ways(up_f, down_f)
    (act_leave,) = call(
        forward_two_kernel, [((1, 1, 3) + small, BF16)], w1, w2, ahead2, embed, masks, out0, out1,
        out=HBM, flops=2 * mm, scratch=out_scratch,
    )
    step_second = adam(part_s, up_s, down_s, m_second, v_second)
    step_first = adam(part_f, up_f, down_f, m_first, v_first)
    return (act_leave, cot_leave, step_first, step_second)


def solution(mesh):
    by_section = P("section", None, None)
    by_rows = P("section", "dp", None)
    by_group = P("dp", "section", None, None)
    ticks = P("dp", "section", None, None, None)
    every = P("dp", None, None, None)
    return jax.shard_map(
        window,
        mesh=mesh,
        in_specs=(by_section, by_section, by_rows, by_rows, by_rows, by_rows, P(),
                  by_group, by_group, every, every, ticks),
        out_specs=(ticks, ticks, by_rows, by_rows),
        check_vma=False,
    )
```

```python
import jax
import jax.numpy as jnp
from jax import lax
from jax.experimental import pallas as pl
from jax.experimental.pallas import tpu as pltpu
from jax.sharding import PartitionSpec as P


D = 512
FF = 2048
ROWS = 256
CHUNK = 512
NORM_EPS = 1e-05
ADAM_EPS = 1e-08
BETA_ONE = 0.9
BETA_TWO = 0.98
CORRECT_ONE = 1.0 - 0.9**10
CORRECT_TWO = 1.0 - 0.98**10
GELU = 0.7978845608
CUBIC = 0.044715
ALPHA = 1500.0**0.25
F32 = jnp.float32
BF16 = jnp.bfloat16

VMEM = pl.BlockSpec(memory_space=pltpu.VMEM)
HBM = pl.BlockSpec(memory_space=pltpu.HBM)


def call(kernel, outs, *args, scratch=(), raw=(), out=VMEM, flops=0, limit=None):
    kernel_call = pl.pallas_call(
        kernel,
        out_shape=[jax.ShapeDtypeStruct(s, d) for s, d in outs],
        in_specs=[HBM if i in raw else VMEM for i in range(len(args))],
        out_specs=[out] * len(outs),
        scratch_shapes=list(scratch),
        cost_estimate=pl.CostEstimate(flops=flops, transcendentals=0, bytes_accessed=0),
        compiler_params=pltpu.CompilerParams(vmem_limit_bytes=limit or (16 << 20)),
    )
    args = [
        pltpu.with_memory_space_constraint(a, pltpu.HBM) if i in raw else a
        for i, a in enumerate(args)
    ]
    return kernel_call(*args)


def dot(a, b):
    return jnp.dot(a, b, preferred_element_type=F32)


def dot_t(a, b):
    return lax.dot_general(a, b, (((1,), (1,)), ((), ())), preferred_element_type=F32)


def chunks(size=CHUNK):
    return [slice(c, c + size) for c in range(0, FF, size)]


def gelu_both(pre):
    w = GELU + (GELU * CUBIC) * (pre * pre)
    a = 0.5 + 0.5 * jnp.tanh(pre * w)
    value = pre * a
    return value, a + value * (1.0 - a) * (6.0 * w - 4.0 * GELU)


def live(length):
    return lax.broadcasted_iota(jnp.int32, (ROWS, 128), 0) < length


def norm_parts(summed):
    center = summed - jnp.mean(summed, axis=1, keepdims=True)
    inv = lax.rsqrt(jnp.mean(center * center, axis=1, keepdims=True) + NORM_EPS)
    return center * inv, inv


def forward_tick(x, w1, w2, mask):
    acc = ALPHA * x.astype(F32)
    columns = chunks(256)
    pre = dot(x, w1[0, :, columns[0]])
    for i, c in enumerate(columns):
        ahead = dot(x, w1[0, :, columns[i + 1]]) if i + 1 < len(columns) else None
        h = gelu_both(pre)[0].astype(BF16)
        acc = acc + dot_t(h, w2[0, :, c])
        pre = ahead
    return jnp.where(mask()[:, :1] > 0.0, norm_parts(acc)[0], 0.0).astype(BF16)


def grad_of_sum(cot, normed, inv_live):
    g = cot.astype(F32)
    mean_g = jnp.mean(g, axis=1, keepdims=True)
    mean_gn = jnp.mean(g * normed, axis=1, keepdims=True)
    return inv_live * (g - mean_g - normed * mean_gn)


def back_zero_kernel(lens_hbm, w1_hbm, w2_hbm, stash_hbm, cot_hbm,
                     gin, gp, h, gs, w1, w2, back_masks, masks,
                     x, slope, cot, lens, sem, w_sem):
    group, section = lax.axis_index("dp"), lax.axis_index("section")
    get_x = pltpu.make_async_copy(stash_hbm.at[0, 0, 0], x, sem.at[0])
    get_x.start()
    streams = [
        [
            pltpu.make_async_copy(src.at[0, :, c], dst.at[0, :, c], w_sem.at[j, i])
            for j, (src, dst) in enumerate(((w1_hbm, w1), (w2_hbm, w2)))
        ]
        for i, c in enumerate(chunks())
    ]
    get_lens = pltpu.make_async_copy(lens_hbm, lens, sem.at[1])
    get_cot = pltpu.make_async_copy(cot_hbm.at[0, 0], cot, sem.at[2])
    for pair in streams[:2]:
        for copy in pair:
            copy.start()
    get_lens.start()
    get_x.wait()
    acc = ALPHA * x[...].astype(F32)
    pre = None
    for i in range(len(streams) + 1):
        if i < len(streams):
            streams[i][0].wait()
            if i + 2 < len(streams):
                streams[i + 2][0].start()
        if i > 0:
            streams[i - 1][1].wait()
            if i + 1 < len(streams):
                streams[i + 1][1].start()
        if i == 1:
            get_cot.start()
        ahead = dot(x[...], w1[0, :, chunks()[i]]) if i < len(streams) else None
        if i > 0:
            c = chunks()[i - 1]
            value, s = gelu_both(pre)
            value = value.astype(BF16)
            h[:, c] = value
            slope[:, c] = s
            acc = acc + dot_t(value, w2[0, :, c])
        pre = ahead
    normed, inv = norm_parts(acc)
    get_lens.wait()
    get_cot.wait()
    inv = jnp.where(live(lens[group, section])[:, :1], inv, 0.0)
    total = grad_of_sum(cot[...], normed, inv)
    total_b = total.astype(BF16)
    gs[...] = total_b
    acc = ALPHA * total
    for c in chunks(1024):
        g = (dot(total_b, w2[0, :, c]) * slope[:, c]).astype(BF16)
        gp[:, c] = g
        acc = acc + dot_t(g, w1[0, :, c])
    gin[...] = acc.astype(BF16)
    last = lax.axis_size("section") - 1
    for k in (1, 2):
        back_masks[k - 1] = live(lens[group, section + k]).astype(F32)
    for k in range(3):
        masks[k] = live(lens[group, last - section + k]).astype(F32)


def prepare(k, w1, w2, stash, masks, h, slope, normed, inv):
    x = stash[0, 0, k]
    acc = ALPHA * x.astype(F32)
    for c in chunks(256):
        value, s = gelu_both(dot(x, w1[0, :, c]))
        value = value.astype(BF16)
        h[:, c] = value
        slope[:, c] = s
        acc = acc + dot_t(value, w2[0, :, c])
    nrm, inv_std = norm_parts(acc)
    normed[...] = nrm
    inv[...] = masks[k - 1] * inv_std


def prepare_one_kernel(*refs):
    prepare(1, *refs)


def prepare_two_kernel(*refs):
    prepare(2, *refs)


def back_one_kernel(w1, w2, passed, loss, slope, normed, inv, gin, gp, gs):
    cot = jnp.where(at_end(), loss[0, 0], passed[...])
    total = grad_of_sum(cot, normed[...], inv[:, :1])
    total_b = total.astype(BF16)
    gs[...] = total_b
    acc = ALPHA * total
    for c in chunks(1024):
        g = (dot(total_b, w2[0, :, c]) * slope[:, c]).astype(BF16)
        gp[:, c] = g
        acc = acc + dot_t(g, w1[0, :, c])
    gin[...] = acc.astype(BF16)


def at_end():
    return lax.axis_index("section") == lax.axis_size("section") - 1


def owner_rows(ref):
    group = lax.axis_index("dp")
    chip, core = group // 2, group % 2
    parts = []
    for which in (core, 1 - core):
        for j in range(4):
            block = 2 * ((chip + j) % 4) + which
            parts.append(ref[pl.ds(pl.multiple_of(block * 64, 64), 64), :])
    return jnp.concatenate(parts, axis=0)


def terms_zero_kernel(stash, gp, gs, h, first, second, x1_rows, x2_rows, left):
    for i, a in enumerate((stash[0, 0, 0], gs[...], stash[0, 0, 1], stash[0, 0, 2])):
        left[i] = jnp.transpose(a)
    a = owner_rows(left.at[0])
    for c in chunks():
        first[:, c] = dot(a, gp[:, c])
    a = owner_rows(left.at[1])
    for c in chunks():
        second[:, c] = dot(a, h[:, c])
    x1_rows[...] = owner_rows(left.at[2])
    x2_rows[...] = owner_rows(left.at[3])


def terms_one_kernel(x_rows, gp, gs, h, first0, second0, first, second, left):
    a = x_rows[...]
    for c in chunks():
        first[:, c] = first0[:, c] + dot(a, gp[:, c])
    left[...] = jnp.transpose(gs[...])
    a = owner_rows(left)
    for c in chunks():
        second[:, c] = second0[:, c] + dot(a, h[:, c])


def back_two_kernel(passed, loss, normed, inv, h2, second, total_out, keep, send, left):
    cot = jnp.where(at_end(), loss[0, 1], passed[...])
    total = grad_of_sum(cot, normed[...], inv[:, :1])
    total_out[...] = total
    left[...] = jnp.transpose(total.astype(BF16))
    a = owner_rows(left)
    for c in chunks():
        r = second[:, c] + dot(a, h2[:, c])
        keep[:, c] = r[:256]
        send[:, c] = r[256:].astype(BF16)


def back_two_first_kernel(w2, total, slope, x_rows, first, gp, keep, send):
    total_b = total[...].astype(BF16)
    a = x_rows[...]
    for c in chunks(1024):
        g = (dot(total_b, w2[0, :, c]) * slope[:, c]).astype(BF16)
        gp[:, c] = g
        r = first[:, c] + dot(a, g)
        keep[:, c] = r[:256]
        send[:, c] = r[256:].astype(BF16)


def leaving(leave, early, last, sem):
    copies = [
        pltpu.make_async_copy(src, leave.at[0, 0, k], sem.at[k])
        for k, src in enumerate(early + (last,))
    ]
    copies[0].start()
    copies[1].start()

    def finish():
        copies[2].start()
        for copy in copies:
            copy.wait()

    return finish


def back_leave_kernel(w1, total, gp, gin0, gin1, leave, gin2, sem):
    finish = leaving(leave, (gin0, gin1), gin2, sem)
    acc = ALPHA * total[...]
    for c in chunks(2048):
        acc = acc + dot_t(gp[:, c], w1[0, :, c])
    gin2[...] = acc.astype(BF16)
    finish()


def forward_zero_kernel(w1, w2, act, masks, out):
    out[...] = forward_tick(act[0, 0], w1, w2, lambda: masks[0])


def forward_one_kernel(w1, w2, passed, embed, masks, out):
    x = jnp.where(lax.axis_index("section") == 0, embed[0, 0], passed[...])
    out[...] = forward_tick(x, w1, w2, lambda: masks[1])


def forward_two_kernel(w1, w2, passed, embed, masks, out0, out1, leave, out2, sem):
    finish = leaving(leave, (out0, out1), out2, sem)
    x = jnp.where(lax.axis_index("section") == 0, embed[0, 1], passed[...])
    out2[...] = forward_tick(x, w1, w2, lambda: masks[2])
    finish()


def ring_start_kernel(keep, got, up, down, mine, later):
    s = [keep[64 * j : 64 * j + 64] + got[64 * j : 64 * j + 64].astype(F32) for j in range(4)]
    up[:32] = s[2][:32].astype(BF16)
    up[32:] = s[1][32:].astype(BF16)
    down[:32] = s[2][32:].astype(BF16)
    down[32:] = s[3][:32].astype(BF16)
    mine[...] = s[0]
    later[:32] = s[1][:32]
    later[32:] = s[3][32:]


def ring_next_kernel(mine, later, got_up, got_down, up, down, part):
    up[...] = (later[:32] + got_up[:32].astype(F32)).astype(BF16)
    down[...] = (later[32:] + got_down[:32].astype(F32)).astype(BF16)
    part[:32] = mine[:32] + got_down[32:].astype(F32)
    part[32:] = mine[32:] + got_up[32:].astype(F32)


def adam_kernel(part, got_up, got_down, m, v, step, new, sem):
    copies = []
    for i in range(4):
        rows, got_rows = slice(16 * i, 16 * i + 16), slice(16 * (i % 2), 16 * (i % 2) + 16)
        g = part[rows] + (got_up, got_down)[i // 2][got_rows].astype(F32)
        m_new = BETA_ONE * m[0, rows] + (1.0 - BETA_ONE) * g
        v_new = BETA_TWO * v[0, rows] + (1.0 - BETA_TWO) * g * g
        new[rows] = m_new / CORRECT_ONE / (jnp.sqrt(v_new / CORRECT_TWO) + ADAM_EPS)
        copies.append(pltpu.make_async_copy(new.at[rows], step.at[0, rows], sem.at[i]))
        copies[i].start()
    for copy in copies:
        copy.wait()


def shifted(x, by, closed=True):
    size = lax.axis_size("section")
    pairs = [(i, (i + by) % size) for i in range(size) if closed or 0 <= i + by < size]
    return lax.ppermute(x, "section", pairs)


def along_x(x, by):
    return lax.ppermute(x, "dp", [(i, ((i // 2 + by) % 4) * 2 + i % 2) for i in range(8)])


def other_core(x):
    return lax.ppermute(x, "dp", [(i, i ^ 1) for i in range(8)])


def window(
    w1, w2, m_first, v_first, m_second, v_second, lens, act, cot, embed, loss, stash
):
    mm = 2 * ROWS * D * FF
    small, wide = (ROWS, D), (ROWS, FF)

    gin0, gp0, h0, gs0, w1, w2, back_masks, masks = call(
        back_zero_kernel,
        [(small, BF16), (wide, BF16), (wide, BF16), (small, BF16), (w1.shape, BF16), (w2.shape, BF16),
         ((2, ROWS, 128), F32), ((3, ROWS, 128), F32)],
        lens, w1, w2, stash, cot, raw=range(5), flops=4 * mm,
        scratch=[pltpu.VMEM(small, BF16), pltpu.VMEM(wide, F32), pltpu.VMEM(small, BF16)]
        + [pltpu.SMEM(lens.shape, jnp.int32), pltpu.SemaphoreType.DMA((3,)),
           pltpu.SemaphoreType.DMA((2, 4))],
    )
    back1 = shifted(gin0, -1)

    def prepared(kernel):
        return call(
            kernel, [(wide, BF16), (wide, F32), (small, F32), ((ROWS, 128), F32)],
            w1, w2, stash, back_masks, flops=2 * mm,
        )

    h1, slope1, normed1, inv1 = prepared(prepare_one_kernel)
    h2, slope2, normed2, inv2 = prepared(prepare_two_kernel)
    acc_first, acc_second, x1_rows, x2_rows = call(
        terms_zero_kernel,
        [((D, FF), F32), ((D, FF), F32), ((D, ROWS), BF16), ((D, ROWS), BF16)],
        stash, gp0, gs0, h0, flops=2 * mm, scratch=[pltpu.VMEM((4, D, ROWS), BF16)],
    )
    gin1, gp1, gs1 = call(
        back_one_kernel, [(small, BF16), (wide, BF16), (small, BF16)],
        w1, w2, back1, loss, slope1, normed1, inv1, flops=2 * mm,
    )
    back2 = shifted(gin1, -1, closed=False)
    (out0,) = call(forward_zero_kernel, [(small, BF16)], w1, w2, act, masks, flops=2 * mm)
    ahead1 = shifted(out0, 1)
    acc_first, acc_second = call(
        terms_one_kernel, [((D, FF), F32), ((D, FF), F32)],
        x1_rows, gp1, gs1, h1, acc_first, acc_second, flops=2 * mm,
        scratch=[pltpu.VMEM((D, ROWS), BF16)],
    )
    total2, keep_second, send_second = call(
        back_two_kernel, [(small, F32), ((256, FF), F32), ((256, FF), BF16)],
        back2, loss, normed2, inv2, h2, acc_second, flops=mm,
        scratch=[pltpu.VMEM((D, ROWS), BF16)],
    )
    got_second = other_core(send_second)
    gp2, keep_first, send_first = call(
        back_two_first_kernel, [(wide, BF16), ((256, FF), F32), ((256, FF), BF16)],
        w2, total2, slope2, x2_rows, acc_first, flops=2 * mm,
    )
    got_first = other_core(send_first)
    (out1,) = call(
        forward_one_kernel, [(small, BF16)], w1, w2, ahead1, embed, masks, flops=2 * mm
    )
    ahead2 = shifted(out1, 1)

    def ring_start(keep, got):
        return call(
            ring_start_kernel,
            [((64, FF), BF16), ((64, FF), BF16), ((64, FF), F32), ((64, FF), F32)], keep, got,
        )

    def ring_next(mine, later, got_up, got_down):
        return call(
            ring_next_kernel, [((32, FF), BF16), ((32, FF), BF16), ((64, FF), F32)],
            mine, later, got_up, got_down,
        )

    def adam(part, got_up, got_down, m, v):
        return call(
            adam_kernel, [((1, 64, FF), F32)], part, got_up, got_down, m, v, out=HBM,
            scratch=[pltpu.VMEM((64, FF), F32), pltpu.SemaphoreType.DMA((4,))],
        )[0]

    def both_ways(up, down):
        up = along_x(up, 1)
        down = along_x(down, -1)
        return up, down

    out_scratch = [pltpu.VMEM(small, BF16), pltpu.SemaphoreType.DMA((3,))]
    up_s, down_s, mine_s, later_s = ring_start(keep_second, got_second)
    up_s, down_s = both_ways(up_s, down_s)
    up_f, down_f, mine_f, later_f = ring_start(keep_first, got_first)
    up_f, down_f = both_ways(up_f, down_f)
    up_s, down_s, part_s = ring_next(mine_s, later_s, up_s, down_s)
    up_s, down_s = both_ways(up_s, down_s)
    (cot_leave,) = call(
        back_leave_kernel, [((1, 1, 3) + small, BF16)], w1, total2, gp2, gin0, gin1,
        out=HBM, flops=mm, scratch=out_scratch,
    )
    up_f, down_f, part_f = ring_next(mine_f, later_f, up_f, down_f)
    up_f, down_f = both_ways(up_f, down_f)
    (act_leave,) = call(
        forward_two_kernel, [((1, 1, 3) + small, BF16)], w1, w2, ahead2, embed, masks, out0, out1,
        out=HBM, flops=2 * mm, scratch=out_scratch,
    )
    step_second = adam(part_s, up_s, down_s, m_second, v_second)
    step_first = adam(part_f, up_f, down_f, m_first, v_first)
    return (act_leave, cot_leave, step_first, step_second)


def solution(mesh):
    by_section = P("section", None, None)
    by_rows = P("section", "dp", None)
    by_group = P("dp", "section", None, None)
    ticks = P("dp", "section", None, None, None)
    every = P("dp", None, None, None)
    return jax.shard_map(
        window,
        mesh=mesh,
        in_specs=(by_section, by_section, by_rows, by_rows, by_rows, by_rows, P(),
                  by_group, by_group, every, every, ticks),
        out_specs=(ticks, ticks, by_rows, by_rows),
        check_vma=False,
    )
```
